128 devices in a mesh: replica: 32 (over z, y, core), shard: 4 (over x).
Axes of the slice: x: 4, y: 4, z: 4, core: 2. Of those that a mesh axis runs over, the one named last changes fastest.
Arguments:
- acts: bfloat16 [2, 65536, 1280], P(None, 'replica', 'shard'), may hold values from -6 to 6
- cots: bfloat16 [2, 65536, 1280], P(None, 'replica'), may hold values from -6 to 6
- errors: float32 [32, 2, 1280, 1280], P('replica', None, 'shard'), may hold values from -4 to 4
- weights: float32 [2, 1280, 1280], P(None, 'shard'), may hold values from -0.3 to 0.3
- momentum: float32 [2, 1280, 1280], P(None, 'shard'), may hold values from -3 to 3
- start_q: float32 [2, 1280, 32], replicated, may hold values from -6 to 6
- vec_grads: float32 [32, 4, 1280], P('replica', None, 'shard'), may hold values from -6 to 6
- vec_weights: float32 [4, 1280], P(None, 'shard'), may hold values from 0.5 to 1.5
- vec_momentum: float32 [4, 1280], P(None, 'shard'), may hold values from -6 to 6
Outputs:
- new_errors: float32 [32, 2, 1280, 1280], P('replica', None, 'shard')
- new_weights: float32 [2, 1280, 1280], P(None, 'shard')
- new_momentum: float32 [2, 1280, 1280], P(None, 'shard')
- new_vec_weights: float32 [4, 1280], P(None, 'shard')
- new_vec_momentum: float32 [4, 1280], P(None, 'shard')
The draws below stay inside these ranges and needn't reach their ends.
All inputs are finite; a program needn't handle non-finite values.
Results may differ from the reference program's by a relative error of at most 0.0003.
Values sent between devices are 32-bit elements; how exact they have to be, the bound alone decides.
No kernel may reach another device: no remote copies, remote signals or barrier semaphores. Data moves between devices by JAX's collectives and lax.ppermute only.
A program may use at most 128 MiB of HBM per device.

```python
import math
import jax
import jax.numpy as jnp
from jax import lax

D = 1280
RANK = 32
NMAT = 2
NVEC = 4
TOK = 2048
REPLICAS = 32
TOKENS = 65536


def signal_parts(key):
    base = jax.random.fold_in(key, 17)
    key_left, key_right, key_coef, key_pick = jax.random.split(base, 4)
    comps = 2 * RANK
    left_dirs = jax.random.normal(key_left, (NMAT, comps, D), jnp.float32)
    right_dirs = jax.random.normal(key_right, (NMAT, comps, D), jnp.float32)
    coef = jax.random.normal(key_coef, (NMAT, TOKENS), jnp.float32)
    picks = jax.random.randint(key_pick, (NMAT, TOKENS), 0, comps)
    ratio = 5.0
    strength = 2.0
    norm_sq = (1.0 - ratio ** (-2.0)) / (1.0 - ratio ** (-2.0 / comps))
    factor = math.sqrt(strength * comps / math.sqrt(norm_sq)) * TOK ** (-0.25)
    position = jnp.arange(comps, dtype=jnp.float32) / comps
    gains = jnp.exp(-0.5 * math.log(ratio) * position) * factor
    picked_gain = gains[picks]
    scale_tok = coef * picked_gain
    return (left_dirs, right_dirs, picks, scale_tok)


def noise_field(key, shape):
    return jax.random.normal(key, shape, jnp.float32)


def pick_rows(table, index):
    return table[index]


def draw_acts(key, part):
    left_dirs, right_dirs, picks, scale_tok = signal_parts(key)
    noise = noise_field(jax.random.fold_in(key, 23), (NMAT, TOKENS, D))
    rows = jax.vmap(pick_rows)(left_dirs, picks)
    return jnp.clip(noise + scale_tok[:, :, None] * rows, -6.0, 6.0).astype(jnp.bfloat16)


def draw_cots(key, part):
    left_dirs, right_dirs, picks, scale_tok = signal_parts(key)
    noise = noise_field(jax.random.fold_in(key, 29), (NMAT, TOKENS, D))
    rows = jax.vmap(pick_rows)(right_dirs, picks)
    return jnp.clip(noise + scale_tok[:, :, None] * rows, -6.0, 6.0).astype(jnp.bfloat16)


def steps_of(own_key, dims, shards, least, high):
    factor_of, own = 1.0, jax.random.fold_in(own_key, 6)
    for dim, shards_of in shards:
        draws = jnp.exp(jax.random.uniform(jax.random.fold_in(own, dim), (shards_of,), jnp.float32, least / len(shards), high / len(shards)))
        factor_of = factor_of * jnp.repeat(draws, dims[dim] // shards_of).reshape([-1 if axis == dim else 1 for axis in range(len(dims))])
    return factor_of


def normal_values(stream_key, extent, width, limit, shards=(), held_as=jnp.bfloat16):
    drawn = jax.random.normal(stream_key, extent, jnp.float32) * width
    if len(shards) > 0:
        drawn = steps_of(stream_key, extent, shards, -0.22, 0.18) * drawn
    return jnp.clip(drawn, min=-limit, max=limit).astype(held_as)


def setup_inputs(seed: int = 0) -> dict:
    key_of = jax.random.split(jax.random.key(seed), 10)
    return {
        "acts": draw_acts(jax.random.fold_in(key_of[9], 71), 0),
        "cots": draw_cots(jax.random.fold_in(key_of[9], 71), 0),
        "errors": normal_values(key_of[2], (REPLICAS, NMAT, D, D), 0.5, 4.0, ((0, 32), (2, 4)), jnp.float32),
        "weights": normal_values(key_of[3], (NMAT, D, D), 0.05, 0.3, ((1, 4),), jnp.float32),
        "momentum": normal_values(key_of[4], (NMAT, D, D), 0.5, 3.0, ((1, 4),), jnp.float32),
        "start_q": normal_values(key_of[5], (NMAT, D, RANK), 1.0, 6.0, (), jnp.float32),
        "vec_grads": normal_values(key_of[6], (REPLICAS, NVEC, D), 1.0, 6.0, ((0, 32), (2, 4)), jnp.float32),
        "vec_weights": jnp.clip(1.0 + 0.1 * jax.random.normal(key_of[7], (NVEC, D), jnp.float32), 0.5, 1.5),
        "vec_momentum": normal_values(key_of[8], (NVEC, D), 1.0, 6.0, ((1, 4),), jnp.float32),
    }


HIGH = lax.Precision.HIGHEST

def orth(block):
    gram = jnp.dot(block.T.astype(jnp.float32), block.astype(jnp.float32), precision=HIGH, preferred_element_type=jnp.float32)
    lower = jnp.linalg.cholesky(gram)
    return lax.linalg.triangular_solve(lower, block, left_side=False, lower=True, transpose_a=True)

def reference(acts, cots, errors, weights, momentum, start_q, vec_grads, vec_weights, vec_momentum):
    scale = 1.0 / math.sqrt(TOK)
    err_list = []
    mom_list = []
    wt_list = []
    for index in range(NMAT):
        inputs = acts[index].reshape(REPLICAS, TOK, D).astype(jnp.float32)
        outputs = cots[index].reshape(REPLICAS, TOK, D).astype(jnp.float32)
        grads = jnp.einsum('rtd,rte->rde', inputs, outputs, precision=HIGH) * scale
        full = grads + errors[:, index]
        right = start_q[index]
        for turn in range(2):
            if turn > 0:
                right = orth(right)
            left = jnp.einsum('rde,ek->dk', full, right, precision=HIGH)
            left = orth(left)
            right = jnp.einsum('rde,dk->ek', full, left, precision=HIGH)
        approx = jnp.dot(left.astype(jnp.float32), right.T.astype(jnp.float32), precision=HIGH, preferred_element_type=jnp.float32) / REPLICAS
        err_list.append(full - approx)
        moved = 0.9 * momentum[index] + approx
        mom_list.append(moved)
        wt_list.append(weights[index] - 0.1 * moved)
    new_errors = jnp.stack(err_list, axis=1)
    vec_moved = 0.9 * vec_momentum + lax.optimization_barrier(jnp.sum(vec_grads, axis=0)) / REPLICAS
    return (new_errors, jnp.stack(wt_list), jnp.stack(mom_list), vec_weights - 0.1 * vec_moved, vec_moved)
```

```python
import math

import jax
import jax.numpy as jnp
from jax import lax
from jax.sharding import PartitionSpec as P

HIGH = lax.Precision.HIGHEST

CORE = [(r, r ^ 1) for r in range(32)]


def y_pairs(k):
    return [(r, r ^ (k << 1)) for r in range(32)]


def z_pairs(k):
    return [(r, r ^ (k << 3)) for r in range(32)]


X_PAIRS = [None] + [[(s, s ^ k) for s in range(4)] for k in (1, 2, 3)]


def swap_y(value, k):
    return lax.ppermute(value, "replica", y_pairs(k))


def swap_z(value, k):
    return lax.ppermute(value, "replica", z_pairs(k))


def swap_x(value, k):
    return lax.ppermute(value, "shard", X_PAIRS[k])


def sum4(value, swap):
    one, two, three = (swap(value, k) for k in (1, 2, 3))
    return (value + one) + (two + three)


def inv_lower(gram):
    lower = jnp.linalg.cholesky(gram)
    eye = jnp.eye(gram.shape[0], dtype=gram.dtype)
    return lax.linalg.triangular_solve(lower, eye, left_side=True, lower=True)


def mm(spec, a, b):
    return jnp.einsum(spec, a, b, precision=HIGH)


def body(acts, cots, errors, weights, momentum, start_q, vec_grads, vec_weights, vec_momentum):
    tok_rows = acts.shape[1]
    rows = acts.shape[2]
    replicas = float(lax.axis_size("replica"))
    index = lax.axis_index("replica")
    core = index & 1
    y = (index >> 1) & 3
    grads = jnp.einsum("mtd,mte->mde", acts, cots, preferred_element_type=jnp.float32)
    full = grads * (1.0 / math.sqrt(tok_rows)) + errors[0]
    own = lax.dynamic_index_in_dim(full, core, 0, False)
    other = lax.dynamic_index_in_dim(full, 1 - core, 0, False)
    both = own + lax.ppermute(other, "replica", CORE)
    parts = both.reshape(rows, 4, -1).transpose(1, 2, 0)
    take = lambda k: lax.dynamic_index_in_dim(parts, y ^ k, 0, False)
    mine = (take(0) + swap_y(take(1), 1)) + (swap_y(take(2), 2) + swap_y(take(3), 3))
    wide = sum4(mine, swap_z)

    q0 = lax.dynamic_index_in_dim(start_q, core, 0, False)
    p1 = sum4(sum4(mm("de,ek->kd", both, q0), swap_y), swap_z)
    vec = sum4(vec_grads[0] + lax.ppermute(vec_grads[0], "replica", CORE), swap_y)
    vec_total = sum4(vec, swap_z)

    packed = jnp.concatenate([mm("ed,kd->ke", wide, p1), mm("kd,ld->kl", p1, p1)], axis=1)
    packed = sum4(packed, swap_x)
    cols = wide.shape[0]
    q1 = mm("lk,ke->le", inv_lower(packed[:, cols:]), packed[:, :cols])

    packed = jnp.concatenate([mm("ke,ed->kd", q1, wide), mm("ke,le->kl", q1, q1)], axis=1)
    packed = sum4(packed, swap_y)
    p2 = mm("lk,kd->ld", inv_lower(packed[:, rows:]), packed[:, :rows])

    packed = jnp.concatenate([mm("ed,kd->ke", wide, p2), mm("kd,ld->kl", p2, p2)], axis=1)
    packed = sum4(packed, swap_x)
    inv = inv_lower(packed[:, cols:])
    left = mm("lk,kd->ld", inv, p2)
    q2 = mm("lk,ke->le", inv, packed[:, :cols])
    quarters = jnp.stack([q2] + [swap_y(q2, k) for k in (1, 2, 3)])
    right = jnp.concatenate([lax.dynamic_index_in_dim(quarters, y ^ k, 0, False) for k in range(4)], axis=1)
    mine = jnp.concatenate([left, right], axis=1)
    theirs = lax.ppermute(mine, "replica", CORE)
    low = jnp.where(core == 0, mine, theirs)
    high = jnp.where(core == 0, theirs, mine)
    pair = jnp.stack([low, high])
    approx = mm("mkd,mke->mde", pair[:, :, :rows], pair[:, :, rows:]) / replicas
    new_errors = (full - approx)[None]
    new_momentum = 0.9 * momentum + approx
    new_weights = weights - 0.1 * new_momentum
    vec_moved = 0.9 * vec_momentum + vec_total / replicas
    return (new_errors, new_weights, new_momentum, vec_weights - 0.1 * vec_moved, vec_moved)


def solution(mesh):
    placed = (
        P(None, "replica", "shard"),
        P(None, "replica", None),
        P("replica", None, "shard", None),
        P(None, "shard", None),
        P(None, "shard", None),
        P(),
        P("replica", None, "shard"),
        P(None, "shard"),
        P(None, "shard"),
    )
    return jax.shard_map(
        body,
        mesh=mesh,
        in_specs=placed,
        out_specs=(
            P("replica", None, "shard", None),
            P(None, "shard", None),
            P(None, "shard", None),
            P(None, "shard"),
            P(None, "shard"),
        ),
        check_vma=False,
    )
```

```python
import math

import jax
import jax.numpy as jnp
from jax import lax
from jax.experimental import pallas as pl
from jax.experimental.pallas import tpu as pltpu
from jax.sharding import PartitionSpec as P

F32 = jnp.float32
BF16 = jnp.bfloat16
HIGH = lax.Precision.HIGHEST
NN = (((1,), (0,)), ((), ()))
NT = (((1,), (1,)), ((), ()))
TN = (((0,), (0,)), ((), ()))

CORE = [(r, r ^ 1) for r in range(32)]


def swap_core(value):
    return lax.ppermute(value, "replica", CORE)


def swap_y(value, k):
    return lax.ppermute(value, "replica", [(r, r ^ (k << 1)) for r in range(32)])


def swap_z(value, k):
    return lax.ppermute(value, "replica", [(r, r ^ (k << 3)) for r in range(32)])


def swap_x(value, k):
    return lax.ppermute(value, "shard", [(s, s ^ k) for s in range(4)])


def fan(value, swap):
    return [value] + [swap(value, k) for k in (1, 2, 3)]


def add4(parts):
    return (parts[0] + parts[1]) + (parts[2] + parts[3])


def dot(a, b, dims, precision=None):
    return lax.dot_general(a, b, dims, precision=precision, preferred_element_type=F32)


def split(value):
    high = value.astype(BF16)
    return high, (value - high.astype(F32)).astype(BF16)


def dot3(a, b_high, b_low, dims):
    high, low = split(a)
    rows = a.shape[0]
    top = dot(jnp.concatenate([high, low], axis=0), b_high, dims)
    return top[:rows] + (top[rows:] + dot(high, b_low, dims))


def lanes(shape):
    return lax.broadcasted_iota(jnp.int32, shape, 1)


def unpack(chunk):
    half = chunk[640:800]
    half = jnp.concatenate([half, pltpu.roll(half, 64, 1)], axis=0)
    half = jnp.where(lanes(half.shape) < 64, half, 0.0)
    return jnp.concatenate([chunk[:320], chunk[320:640], half], axis=1)


def grad_kernel(which, a_ref, c_ref, e_ref, out_ref, *, scale):
    out_ref[...] = dot(a_ref[0], c_ref[0], NN) * scale + e_ref[0]


def route_kernel(where, a_ref, b_ref, o0, o1, o2, o3, stage):
    left = lanes((160, 128)) < 64
    for i in range(2):
        def tile(t):
            at = 640 * i + 128 * t
            return a_ref[:, at:at + 128] + b_ref[:, at:at + 128]
        middle = tile(2)
        rolled = pltpu.roll(middle, 64, 1)
        stage[2 * i, 0:320] = tile(0)
        stage[2 * i, 320:640] = tile(1)
        stage[2 * i, 640:800] = jnp.where(left, middle[:160], rolled[160:])
        stage[2 * i + 1, 0:320] = tile(3)
        stage[2 * i + 1, 320:640] = tile(4)
        stage[2 * i + 1, 640:800] = jnp.where(left, rolled[:160], middle[160:])
    y = where[1]
    for k, out in enumerate((o0, o1, o2, o3)):
        out[...] = stage[y ^ k]


def first_kernel(where, c0, c1, c2, c3, q_ref, v_ref, out_ref, stage):
    core, y = where[0], where[1]
    q = q_ref[core]
    left = lanes((32, 128)) < 64
    for i in range(2):
        at = 640 * i
        middle = q[:, at + 256:at + 384]
        stage[2 * i, :, 0:256] = q[:, at:at + 256]
        stage[2 * i, :, 256:384] = jnp.where(left, middle, 0.0)
        stage[2 * i + 1, :, 0:256] = q[:, at + 384:at + 640]
        stage[2 * i + 1, :, 256:384] = jnp.where(left, pltpu.roll(middle, 64, 1), 0.0)
    total = jnp.zeros((32, 320), F32)
    for k, chunk in enumerate((c0, c1, c2, c3)):
        high, low = split(unpack(chunk[...]))
        total = total + dot3(stage[y ^ k], high, low, NT)
    out_ref[...] = jnp.zeros((40, 384), F32)
    out_ref[0:32, 0:320] = total
    out_ref[32:36, 0:320] = v_ref[...]


def eliminate(tile):
    lane = lanes((32, 128))
    row = lax.broadcasted_iota(jnp.int32, (32, 128), 0)
    work = jnp.where((lane >= 64) & (lane < 96), tile, jnp.where(lane == row + 96, 1.0, 0.0))
    for k in range(31):
        factor = work[:, 64 + k:65 + k] * (1.0 / work[k:k + 1, 64 + k:65 + k])
        work = work - jnp.where(row > k, factor * work[k:k + 1, :], 0.0)
    pivots = jnp.sum(jnp.where(lane == row + 64, work, 0.0), axis=1, keepdims=True)
    return jnp.where(lane >= 96, work, 0.0), pivots


def below(value):
    return jnp.concatenate([jnp.zeros((96, value.shape[1]), F32), value], axis=0)


def payload(value):
    return jnp.where(lanes(value.shape) < 320, value, 0.0)


def orth(packed):
    inverse, pivots = eliminate(packed[:, 256:384])
    return dot(inverse * lax.rsqrt(pivots), below(payload(packed)), NN, HIGH)


def to_right(left, w_high, w_low):
    out = dot3(left, w_high, w_low, NN)
    zero = jnp.zeros((64, left.shape[1]), F32)
    shifted = jnp.concatenate([zero, left, zero[:32]], axis=0)
    gram = dot(left, shifted, NT, HIGH)
    return jnp.concatenate([out[:, :256], out[:, 256:] + gram], axis=1)


def wide_kernel(m0, m1, m2, m3, p0, p1, p2, p3, high_ref, low_ref, out_ref):
    whole = unpack((m0[...] + m1[...]) + (m2[...] + m3[...]))
    high, low = split(whole)
    zero = jnp.zeros((64, 384), BF16)
    high_ref[...] = jnp.concatenate([high, zero], axis=0)
    low_ref[...] = jnp.concatenate([low, zero], axis=0)
    left = ((p0[...] + p1[...]) + (p2[...] + p3[...]))[:32]
    out_ref[...] = to_right(left, high_ref[...], low_ref[...])


def left_kernel(a0, a1, a2, a3, high_ref, low_ref, out_ref):
    right = orth((a0[...] + a1[...]) + (a2[...] + a3[...]))
    high, low = split(right)
    zero = jnp.zeros((32, 384), BF16)
    w_high = jnp.concatenate([high_ref[0:320], high, zero], axis=0)
    w_low = jnp.concatenate([low_ref[0:320], low, zero], axis=0)
    out_ref[...] = dot3(right, w_high, w_low, NT)


def right_kernel(a0, a1, a2, a3, high_ref, low_ref, left_ref, out_ref):
    left = orth((a0[...] + a1[...]) + (a2[...] + a3[...]))
    left_ref[...] = left
    out_ref[...] = to_right(left, high_ref[...], low_ref[...])


def solve_kernel(packed_ref, left_ref, out_ref, *, scale):
    inverse, pivots = eliminate(packed_ref[:, 256:384])
    once = dot(inverse, below(left_ref[...]), NN, HIGH) * (scale / pivots)
    out_ref[...] = dot(inverse, once, TN, HIGH)[96:128]


def final_kernel(where, own, other, g0, g1, g2, g3, l_own, l_other, w_ref, m_ref,
                 e_out, w_out, m_out, stage, approx):
    slot, block = pl.program_id(0), pl.program_id(1)
    y = where[1]

    def start(first, left_ref):
        for k, g in enumerate((g0, g1, g2, g3)):
            stage[y ^ k] = g[first:first + 32]
        side = lanes((32, 128)) < 64
        tiles = []
        for i in range(2):
            even, odd = stage[2 * i], stage[2 * i + 1]
            middle = jnp.where(side, even[:, 256:], pltpu.roll(odd[:, 256:], 64, 1))
            tiles += [even[:, :256], middle, odd[:, :256]]
        r_high, r_low = split(jnp.concatenate(tiles, axis=1))
        l_high, l_low = split(left_ref[...])
        rights = jnp.concatenate([r_high, r_low, r_high], axis=0)
        lefts = jnp.concatenate([l_high, l_high, l_low], axis=0)
        approx[...] = dot(lefts, rights, TN)[:320]

    @pl.when((slot == 0) & (block == 0))
    def _():
        start(0, l_own)

    @pl.when((slot == 1) & (block == 0))
    def _():
        start(32, l_other)

    size = w_ref.shape[1]
    at = pl.multiple_of(block * size, 8)
    part = approx[pl.ds(at, size), :]

    @pl.when(slot == 0)
    def _():
        e_out[0] = own[pl.ds(at, size), :] - part

    @pl.when(slot == 1)
    def _():
        e_out[0] = other[pl.ds(at, size), :] - part

    moved = 0.9 * m_ref[0] + part
    m_out[0] = moved
    w_out[0] = w_ref[0] - 0.1 * moved


VM = pl.BlockSpec(memory_space=pltpu.VMEM)
SM = pl.BlockSpec(memory_space=pltpu.SMEM)
LIMIT = pltpu.CompilerParams(vmem_limit_bytes=40 << 20)


def shaped(shape, dtype=F32):
    return jax.ShapeDtypeStruct(shape, dtype)


def call(kernel, args, outs, specs, scratch=(), name=None):
    many = isinstance(outs, (list, tuple))
    return pl.pallas_call(
        kernel,
        out_shape=outs,
        in_specs=specs,
        out_specs=[VM] * len(outs) if many else VM,
        scratch_shapes=list(scratch),
        compiler_params=LIMIT,
        name=name,
    )(*args)


def gradients(which, acts, cots, errors, scale, name):
    mats, rows, toks = acts.shape
    cols = cots.shape[2]
    step = 256
    return pl.pallas_call(
        lambda *refs: grad_kernel(*refs, scale=scale),
        out_shape=shaped((rows, cols)),
        grid_spec=pltpu.PrefetchScalarGridSpec(
            num_scalar_prefetch=1,
            grid=(cols // step,),
            in_specs=[
                pl.BlockSpec((1, rows, toks), lambda j, s: (s[0], 0, 0)),
                pl.BlockSpec((1, toks, step), lambda j, s: (s[0], 0, j)),
                pl.BlockSpec((1, rows, step), lambda j, s: (s[0], 0, j)),
            ],
            out_specs=pl.BlockSpec((rows, step), lambda j, s: (0, j)),
        ),
        compiler_params=LIMIT,
        name=name,
    )(which, acts, cots, errors)


def finish(where, own, other, rights, l_own, l_other, weights, momentum):
    mats, rows, cols = weights.shape
    blocks = 4
    size = rows // blocks
    block = pl.BlockSpec((1, size, cols), lambda s, i, w: (w[0] ^ s, i, 0))
    return pl.pallas_call(
        final_kernel,
        out_shape=[shaped(weights.shape)] * 3,
        grid_spec=pltpu.PrefetchScalarGridSpec(
            num_scalar_prefetch=1,
            grid=(mats, blocks),
            in_specs=[VM] * 8 + [block, block],
            out_specs=[block] * 3,
            scratch_shapes=[pltpu.VMEM((4, 32, 384), F32), pltpu.VMEM((rows, cols), F32)],
        ),
        compiler_params=LIMIT,
        name="finish",
    )(where, own, other, *rights, l_own, l_other, weights, momentum)


def body(acts, cots, errors, weights, momentum, start_q, vec_grads, vec_weights, vec_momentum):
    scale = 1.0 / math.sqrt(acts.shape[1])
    replicas = float(lax.axis_size("replica"))
    index = lax.axis_index("replica")
    core = index & 1
    y = (index >> 1) & 3
    where = jnp.stack([core, y]).astype(jnp.int32)
    acts = acts.swapaxes(1, 2)

    vec_core = vec_grads[0] + swap_core(vec_grads[0])
    other = gradients(1 - where[:1], acts, cots, errors[0], scale, "grad_other")
    own = gradients(where[:1], acts, cots, errors[0], scale, "grad_own")
    chunks = call(route_kernel, (where, own, swap_core(other)), [shaped((800, 128))] * 4, [SM, VM, VM],
                  [pltpu.VMEM((4, 800, 128), F32)], name="route")
    mine = add4([chunks[0]] + [swap_y(chunks[k], k) for k in (1, 2, 3)])
    first = call(first_kernel, (where, *chunks, start_q.swapaxes(1, 2), vec_core), shaped((40, 384)),
                 [SM] + [VM] * 6, [pltpu.VMEM((4, 32, 384), F32)], name="first_left")
    firsts = fan(add4(fan(first, swap_y)), swap_z)
    wides = fan(mine, swap_z)
    w_high, w_low, packed = call(wide_kernel, (*wides, *firsts),
                                 [shaped((384, 384), BF16), shaped((384, 384), BF16), shaped((32, 384))],
                                 [VM] * 8, name="first_right")
    packed = call(left_kernel, (*fan(packed, swap_x), w_high, w_low), shaped((32, 384)), [VM] * 6, name="second_left")
    left, packed = call(right_kernel, (*fan(packed, swap_y), w_high, w_low), [shaped((32, 384))] * 2, [VM] * 6,
                        name="second_right")
    packed = add4(fan(packed, swap_x))
    rights = fan(jnp.concatenate([packed, swap_core(packed)], axis=0), swap_y)
    l_own = call(lambda *refs: solve_kernel(*refs, scale=1.0 / replicas), (packed, left), shaped((32, 384)), [VM] * 2,
                 name="solve")
    new_errors, new_weights, new_momentum = finish(where, own, other, rights, l_own, swap_core(l_own), weights, momentum)
    vec_moved = 0.9 * vec_momentum + add4(firsts)[32:36, :320] / replicas
    return (new_errors[None], new_weights, new_momentum, vec_weights - 0.1 * vec_moved, vec_moved)


def solution(mesh):
    placed = (
        P(None, "replica", "shard"),
        P(None, "replica", None),
        P("replica", None, "shard", None),
        P(None, "shard", None),
        P(None, "shard", None),
        P(),
        P("replica", None, "shard"),
        P(None, "shard"),
        P(None, "shard"),
    )
    return jax.shard_map(
        body,
        mesh=mesh,
        in_specs=placed,
        out_specs=(
            P("replica", None, "shard", None),
            P(None, "shard", None),
            P(None, "shard", None),
            P(None, "shard"),
            P(None, "shard"),
        ),
        check_vma=False,
    )
```

```python
import math

import jax
import jax.numpy as jnp
from jax import lax
from jax.experimental import pallas as pl
from jax.experimental.pallas import tpu as pltpu
from jax.sharding import PartitionSpec as P

F32 = jnp.float32
BF16 = jnp.bfloat16
HIGH = lax.Precision.HIGHEST
NN = (((1,), (0,)), ((), ()))
NT = (((1,), (1,)), ((), ()))
TN = (((0,), (0,)), ((), ()))

CORE = [(r, r ^ 1) for r in range(32)]


def swap_core(value):
    return lax.ppermute(value, "replica", CORE)


def swap_y(value, k):
    return lax.ppermute(value, "replica", [(r, r ^ (k << 1)) for r in range(32)])


def swap_z(value, k):
    return lax.ppermute(value, "replica", [(r, r ^ (k << 3)) for r in range(32)])


def swap_x(value, k):
    return lax.ppermute(value, "shard", [(s, s ^ k) for s in range(4)])


def fan(value, swap):
    return [value] + [swap(value, k) for k in (1, 2, 3)]


def add4(parts):
    return (parts[0] + parts[1]) + (parts[2] + parts[3])


def dot(a, b, dims, precision=None):
    return lax.dot_general(a, b, dims, precision=precision, preferred_element_type=F32)


def split(value):
    high = value.astype(BF16)
    return high, (value - high.astype(F32)).astype(BF16)


def dot3(a, b_high, b_low, dims):
    high, low = split(a)
    rows = a.shape[0]
    top = dot(jnp.concatenate([high, low], axis=0), b_high, dims)
    return top[:rows] + (top[rows:] + dot(high, b_low, dims))


def lanes(shape):
    return lax.broadcasted_iota(jnp.int32, shape, 1)


def unpack(chunk):
    half = chunk[640:800]
    half = jnp.concatenate([half, pltpu.roll(half, 64, 1)], axis=0)
    half = jnp.where(lanes(half.shape) < 64, half, 0.0)
    return jnp.concatenate([chunk[:320], chunk[320:640], half], axis=1)


def grad_kernel(which, a_hbm, c_hbm, e_hbm, out_ref, a_buf, c_buf, e_buf, a_sem, c_sem, e_sem, *, scale, step, ahead):
    mat = which[0]
    blocks = [pl.ds(at, step) for at in range(0, c_buf.shape[0], step)]
    lhs = [pltpu.make_async_copy(a_hbm.at[mat, :, b], a_buf.at[:, b], a_sem.at[j]) for j, b in enumerate(blocks)]
    rhs = [pltpu.make_async_copy(c_hbm.at[mat, b], c_buf.at[b], c_sem.at[j]) for j, b in enumerate(blocks)]
    kept = pltpu.make_async_copy(e_hbm.at[mat], e_buf, e_sem)
    last = len(blocks) - 1

    def start(j):
        if j <= last:
            lhs[j].start()
            rhs[j].start()
        if j == last:
            kept.start()

    for j in range(ahead):
        start(j)
    for j, b in enumerate(blocks):
        lhs[j].wait()
        rhs[j].wait()
        start(j + ahead)
        value = dot(a_buf[:, b], c_buf[b], NN)
        if j == last:
            kept.wait()
            out_ref[...] = (out_ref[...] + value) * scale + e_buf[...]
        elif j > 0:
            out_ref[...] = out_ref[...] + value
        else:
            out_ref[...] = value


AHEAD = 448
REST = 800 - AHEAD


def route_kernel(where, a_ref, b_ref, q_hbm, v_ref, o0, o1, o2, o3, r0, r1, r2, r3, stage, both, q_buf, q_sem):
    core, y = where[0], where[1]
    fetch = pltpu.make_async_copy(q_hbm.at[core], q_buf, q_sem)
    fetch.start()
    left = lanes((160, 128)) < 64
    for i in range(2):
        tiles = []
        for t in range(5):
            at = 640 * i + 128 * t
            tiles.append(a_ref[:, at:at + 128] + b_ref[:, at:at + 128])
            both[0:320, at:at + 128] = tiles[-1]
        middle = tiles[2]
        rolled = pltpu.roll(middle, 64, 1)
        stage[2 * i, 0:320] = tiles[0]
        stage[2 * i, 320:640] = tiles[1]
        stage[2 * i, 640:800] = jnp.where(left, middle[:160], rolled[160:])
        stage[2 * i + 1, 0:320] = tiles[3]
        stage[2 * i + 1, 320:640] = tiles[4]
        stage[2 * i + 1, 640:800] = jnp.where(left, rolled[:160], middle[160:])
    both[320:384] = jnp.zeros((64, both.shape[1]), F32)
    for k, (out, rest) in enumerate(((o0, r0), (o1, r1), (o2, r2), (o3, r3))):
        out[...] = stage[y ^ k, 0:AHEAD]
        rest[0:REST] = stage[y ^ k, AHEAD:800]
    fetch.wait()
    high, low = split(both[...])
    total = dot3(q_buf[...], high, low, NT)
    for rest in (r0, r1, r2, r3):
        rest[REST:REST + 32] = total[:, 0:128]
        rest[REST + 32:REST + 64] = total[:, 128:256]
        rest[REST + 64:REST + 96] = total[:, 256:384] + v_ref[...]


def eliminate(tile):
    lane = lanes((32, 128))
    row = lax.broadcasted_iota(jnp.int32, (32, 128), 0)
    gram = jnp.where((lane >= 64) & (lane < 96), tile, 0.0)
    diagonal = jnp.where(lane == row + 64, gram, 0.0)
    down = lax.rsqrt(jnp.sum(diagonal, axis=1, keepdims=True))
    across = jnp.sum(diagonal, axis=0, keepdims=True)
    across = lax.rsqrt(jnp.where((lane[0:1] >= 64) & (lane[0:1] < 96), across, 1.0))
    work = gram * down * across + jnp.where(lane == row + 96, down, 0.0)
    for k in range(0, 32, 2):
        col0 = jnp.broadcast_to(work[:, 64 + k:65 + k], (32, 128))
        col1 = jnp.broadcast_to(work[:, 65 + k:66 + k], (32, 128))
        a, b, c = col0[k:k + 1], col0[k + 1:k + 2], col1[k + 1:k + 2]
        row0, row1 = work[k:k + 1], work[k + 1:k + 2]
        inverse = 1.0 / (a * c - b * b)
        step0 = (c * row0 - b * row1) * inverse
        step1 = (a * row1 - b * row0) * inverse
        second = jnp.where(row == k + 1, (b * (1.0 / a)) * row0, 0.0)
        work = work - jnp.where(row > k + 1, col0 * step0 + col1 * step1, second)
    pivots = jnp.sum(jnp.where(lane == row + 64, work, 0.0), axis=1, keepdims=True)
    return jnp.where(lane >= 96, work, 0.0), pivots


def below(value):
    return jnp.concatenate([jnp.zeros((96, value.shape[1]), F32), value], axis=0)


def payload(value):
    return jnp.where(lanes(value.shape) < 320, value, 0.0)


def orth(packed):
    inverse, pivots = eliminate(packed[:, 256:384])
    return dot(inverse * lax.rsqrt(pivots), below(payload(packed)), NN, HIGH)


def to_right(left, w_high, w_low):
    out = dot3(left, w_high, w_low, NN)
    zero = jnp.zeros((64, left.shape[1]), F32)
    shifted = jnp.concatenate([zero, left, zero[:32]], axis=0)
    gram = dot(left, shifted, NT, HIGH)
    return jnp.concatenate([out[:, :256], out[:, 256:] + gram], axis=1)


def wide_kernel(m0, m1, m2, m3, p0, p1, p2, p3, high_ref, low_ref, out_ref, vec_ref):
    tail = (p0[...] + p1[...]) + (p2[...] + p3[...])
    whole = unpack(jnp.concatenate([(m0[...] + m1[...]) + (m2[...] + m3[...]), tail[:REST]], axis=0))
    high, low = split(whole)
    zero = jnp.zeros((64, 384), BF16)
    high_ref[...] = jnp.concatenate([high, zero], axis=0)
    low_ref[...] = jnp.concatenate([low, zero], axis=0)
    vec_ref[...] = tail[REST + 64:REST + 96]
    left = payload(jnp.concatenate([tail[REST:REST + 32], tail[REST + 32:REST + 64], tail[REST + 64:REST + 96]], axis=1))
    out_ref[...] = to_right(left, high_ref[...], low_ref[...])


def left_kernel(a0, a1, a2, a3, high_ref, low_ref, out_ref):
    right = orth((a0[...] + a1[...]) + (a2[...] + a3[...]))
    high, low = split(right)
    zero = jnp.zeros((32, 384), BF16)
    w_high = jnp.concatenate([high_ref[0:320], high, zero], axis=0)
    w_low = jnp.concatenate([low_ref[0:320], low, zero], axis=0)
    out_ref[...] = dot3(right, w_high, w_low, NT)


def right_kernel(a0, a1, a2, a3, high_ref, low_ref, left_ref, out_ref):
    left = orth((a0[...] + a1[...]) + (a2[...] + a3[...]))
    left_ref[...] = left
    out_ref[...] = to_right(left, high_ref[...], low_ref[...])


def solve_kernel(packed_ref, left_ref, w_hbm, m_hbm, out_ref, w_out, m_out, sems, *, scale):
    one = pltpu.make_async_copy(w_hbm, w_out, sems.at[0])
    two = pltpu.make_async_copy(m_hbm, m_out, sems.at[1])
    one.start()
    two.start()
    inverse, pivots = eliminate(packed_ref[0:32, 256:384])
    once = dot(inverse, below(left_ref[...]), NN, HIGH) * (scale / pivots)
    out_ref[...] = dot(inverse, once, TN, HIGH)[96:128]
    one.wait()
    two.wait()


def final_kernel(where, own, other, g0, g1, g2, g3, l_own, l_other, w_ref, m_ref,
                 e_hbm, w_hbm, m_hbm, stage, e_buf, w_buf, m_buf, sems, *, blocks):
    core, y = where[0], where[1]
    size = own.shape[0] // blocks
    side = lanes((32, 128)) < 64
    copies = []
    for slot, (full, left_ref) in enumerate(((own, l_own), (other, l_other))):
        mat = core ^ slot
        for k, g in enumerate((g0, g1, g2, g3)):
            stage[y ^ k] = g[32 * slot:32 * slot + 32]
        tiles = []
        for i in range(2):
            even, odd = stage[2 * i], stage[2 * i + 1]
            middle = jnp.where(side, even[:, 256:], pltpu.roll(odd[:, 256:], 64, 1))
            tiles += [even[:, :256], middle, odd[:, :256]]
        r_high, r_low = split(jnp.concatenate(tiles, axis=1))
        l_high, l_low = split(left_ref[...])
        rights = jnp.concatenate([r_high, r_low, r_high], axis=0)
        lefts = jnp.concatenate([l_high, l_high, l_low], axis=0).T
        for block in range(blocks):
            rows = slice(block * size, block * size + size)
            part = dot(lefts[rows], rights, NN)
            e_buf[slot, rows] = full[rows] - part
            moved = 0.9 * m_ref[mat, rows] + part
            m_buf[slot, rows] = moved
            w_buf[slot, rows] = w_ref[mat, rows] - 0.1 * moved
            for j, (buf, hbm) in enumerate(((e_buf, e_hbm), (m_buf, m_hbm), (w_buf, w_hbm))):
                copies.append(pltpu.make_async_copy(buf.at[slot, rows], hbm.at[mat, rows], sems.at[slot, block, j]))
                copies[-1].start()
    for copy in copies:
        copy.wait()


VM = pl.BlockSpec(memory_space=pltpu.VMEM)
SM = pl.BlockSpec(memory_space=pltpu.SMEM)


def limit(mebi):
    return pltpu.CompilerParams(vmem_limit_bytes=mebi << 20)


def shaped(shape, dtype=F32):
    return jax.ShapeDtypeStruct(shape, dtype)


def call(kernel, args, outs, specs, scratch=(), name=None):
    many = isinstance(outs, (list, tuple))
    return pl.pallas_call(
        kernel,
        out_shape=outs,
        in_specs=specs,
        out_specs=[VM] * len(outs) if many else VM,
        scratch_shapes=list(scratch),
        compiler_params=limit(12),
        name=name,
    )(*args)


def gradients(which, acts, cots, errors, scale, name):
    mats, rows, toks = acts.shape
    cols = cots.shape[2]
    step = 512
    inputs = [pltpu.with_memory_space_constraint(value, pltpu.HBM) for value in (acts, cots, errors)]
    return pl.pallas_call(
        lambda *refs: grad_kernel(*refs, scale=scale, step=step, ahead=3),
        out_shape=shaped((rows, cols)),
        in_specs=[SM] + [pl.BlockSpec(memory_space=pltpu.HBM)] * 3,
        out_specs=VM,
        scratch_shapes=[
            pltpu.VMEM((rows, toks), BF16),
            pltpu.VMEM((toks, cols), BF16),
            pltpu.VMEM((rows, cols), F32),
            pltpu.SemaphoreType.DMA((toks // step,)),
            pltpu.SemaphoreType.DMA((toks // step,)),
            pltpu.SemaphoreType.DMA(()),
        ],
        compiler_params=limit(16),
        name=name,
    )(which, *inputs)


def finish(where, own, other, rights, l_own, l_other, weights, momentum):
    blocks = 4
    hbm = pl.BlockSpec(memory_space=pltpu.HBM)
    return pl.pallas_call(
        lambda *refs: final_kernel(*refs, blocks=blocks),
        out_shape=[shaped(weights.shape)] * 3,
        in_specs=[SM] + [VM] * 10,
        out_specs=[hbm] * 3,
        scratch_shapes=[pltpu.VMEM((4, 32, 384), F32)] + [pltpu.VMEM(weights.shape, F32)] * 3
        + [pltpu.SemaphoreType.DMA((2, blocks, 3))],
        compiler_params=limit(24),
        name="finish",
    )(where, own, other, *rights, l_own, l_other, weights, momentum)


def body(acts, cots, errors, weights, momentum, start_q, vec_grads, vec_weights, vec_momentum):
    scale = 1.0 / math.sqrt(acts.shape[1])
    replicas = float(lax.axis_size("replica"))
    index = lax.axis_index("replica")
    core = index & 1
    y = (index >> 1) & 3
    where = jnp.stack([core, y]).astype(jnp.int32)
    acts = acts.swapaxes(1, 2)

    vec_core = vec_grads[0] + swap_core(vec_grads[0])
    other = gradients(1 - where[:1], acts, cots, errors[0], scale, "grad_other")
    own = gradients(where[:1], acts, cots, errors[0], scale, "grad_own")
    vec_core = jnp.pad(vec_core.reshape(20, 64), ((0, 12), (64, 0)))
    hbm = pl.BlockSpec(memory_space=pltpu.HBM)
    in_hbm = lambda value: pltpu.with_memory_space_constraint(value, pltpu.HBM)
    sends = call(route_kernel, (where, own, swap_core(other), in_hbm(start_q.swapaxes(1, 2)), vec_core),
                 [shaped((AHEAD, 128))] * 4 + [shaped((REST + 96, 128))] * 4, [SM, VM, VM, hbm, VM],
                 [pltpu.VMEM((4, 800, 128), F32), pltpu.VMEM((384, 1280), F32), pltpu.VMEM((32, 1280), F32),
                  pltpu.SemaphoreType.DMA(())], name="route")
    ahead = add4([sends[0]] + [swap_y(sends[k], k) for k in (1, 2, 3)])
    behind = add4([sends[4]] + [swap_y(sends[4 + k], k) for k in (1, 2, 3)])
    w_high, w_low, packed, vec_sum = call(
        wide_kernel, (*fan(ahead, swap_z), *fan(behind, swap_z)),
        [shaped((384, 384), BF16), shaped((384, 384), BF16), shaped((32, 384)), shaped((32, 128))],
        [VM] * 8, name="first_right")
    packed = call(left_kernel, (*fan(packed, swap_x), w_high, w_low), shaped((32, 384)), [VM] * 6, name="second_left")
    left, packed = call(right_kernel, (*fan(packed, swap_y), w_high, w_low), [shaped((32, 384))] * 2, [VM] * 6,
                        name="second_right")
    packed = add4(fan(packed, swap_x))
    rights = fan(jnp.concatenate([packed, swap_core(packed)], axis=0), swap_y)
    held = pltpu.VMEM(weights.shape, F32)
    l_own, weights, momentum = call(
        lambda *refs: solve_kernel(*refs, scale=1.0 / replicas), (rights[0], left, in_hbm(weights), in_hbm(momentum)),
        [shaped((32, 384)), held, held], [VM, VM, hbm, hbm], [pltpu.SemaphoreType.DMA((2,))], name="solve")
    new_errors, new_weights, new_momentum = finish(where, own, other, rights, l_own, swap_core(l_own), weights, momentum)
    vec_moved = 0.9 * vec_momentum + vec_sum[:20, 64:].reshape(4, 320) / replicas
    return (new_errors[None], new_weights, new_momentum, vec_weights - 0.1 * vec_moved, vec_moved)


def solution(mesh):
    placed = (
        P(None, "replica", "shard"),
        P(None, "replica", None),
        P("replica", None, "shard", None),
        P(None, "shard", None),
        P(None, "shard", None),
        P(),
        P("replica", None, "shard"),
        P(None, "shard"),
        P(None, "shard"),
    )
    return jax.shard_map(
        body,
        mesh=mesh,
        in_specs=placed,
        out_specs=(
            P("replica", None, "shard", None),
            P(None, "shard", None),
            P(None, "shard", None),
            P(None, "shard"),
            P(None, "shard"),
        ),
        check_vma=False,
    )
```

```python
import math

import jax
import jax.numpy as jnp
from jax import lax
from jax.experimental import pallas as pl
from jax.experimental.pallas import tpu as pltpu
from jax.sharding import PartitionSpec as P

F32 = jnp.float32
BF16 = jnp.bfloat16
HIGH = lax.Precision.HIGHEST
NN = (((1,), (0,)), ((), ()))
NT = (((1,), (1,)), ((), ()))
TN = (((0,), (0,)), ((), ()))

CORE = [(r, r ^ 1) for r in range(32)]


def swap_core(value):
    return lax.ppermute(value, "replica", CORE)


def swap_y(value, k):
    return lax.ppermute(value, "replica", [(r, r ^ (k << 1)) for r in range(32)])


def swap_z(value, k):
    return lax.ppermute(value, "replica", [(r, r ^ (k << 3)) for r in range(32)])


def swap_x(value, k):
    return lax.ppermute(value, "shard", [(s, s ^ k) for s in range(4)])


def fan(value, swap):
    return [value] + [swap(value, k) for k in (1, 2, 3)]


def add4(parts):
    return (parts[0] + parts[1]) + (parts[2] + parts[3])


def dot(a, b, dims, precision=None):
    return lax.dot_general(a, b, dims, precision=precision, preferred_element_type=F32)


def split(value):
    high = value.astype(BF16)
    return high, (value - high.astype(F32)).astype(BF16)


def dot3(a, b_high, b_low, dims):
    high, low = split(a)
    rows = a.shape[0]
    top = dot(jnp.concatenate([high, low], axis=0), b_high, dims)
    return top[:rows] + (top[rows:] + dot(high, b_low, dims))


def lanes(shape):
    return lax.broadcasted_iota(jnp.int32, shape, 1)


def unpack(chunk):
    half = chunk[640:800]
    half = jnp.concatenate([half, pltpu.roll(half, 64, 1)], axis=0)
    half = jnp.where(lanes(half.shape) < 64, half, 0.0)
    return jnp.concatenate([chunk[:320], chunk[320:640], half], axis=1)


def grad_kernel(which, a_hbm, c_hbm, e_hbm, out_ref, a_buf, c_buf, e_buf, a_sem, c_sem, e_sem, *, scale, step, ahead):
    mat = which[0]
    blocks = [pl.ds(at, step) for at in range(0, c_buf.shape[0], step)]
    lhs = [pltpu.make_async_copy(a_hbm.at[mat, :, b], a_buf.at[:, b], a_sem.at[j]) for j, b in enumerate(blocks)]
    rhs = [pltpu.make_async_copy(c_hbm.at[mat, b], c_buf.at[b], c_sem.at[j]) for j, b in enumerate(blocks)]
    kept = pltpu.make_async_copy(e_hbm.at[mat], e_buf, e_sem)
    last = len(blocks) - 1

    def start(j):
        if j <= last:
            lhs[j].start()
            rhs[j].start()
        if j == last:
            kept.start()

    for j in range(ahead):
        start(j)
    for j, b in enumerate(blocks):
        lhs[j].wait()
        rhs[j].wait()
        start(j + ahead)
        value = dot(a_buf[:, b], c_buf[b], NN)
        if j == last:
            kept.wait()
            out_ref[...] = (out_ref[...] + value) * scale + e_buf[...]
        elif j > 0:
            out_ref[...] = out_ref[...] + value
        else:
            out_ref[...] = value


AHEAD = 448
REST = 800 - AHEAD


def route_kernel(where, a_ref, b_hbm, q_hbm, v_ref, o0, o1, o2, o3, r0, r1, r2, r3, stage, both, b_ref, q_buf, b_sem, q_sem):
    core, y = where[0], where[1]
    fetch = pltpu.make_async_copy(q_hbm.at[core], q_buf, q_sem)
    halves = [pltpu.make_async_copy(b_hbm.at[:, at:at + 640], b_ref.at[:, at:at + 640], b_sem.at[i])
              for i, at in enumerate((0, 640))]
    halves[0].start()
    halves[1].start()
    fetch.start()
    left = lanes((160, 128)) < 64
    for i in range(2):
        halves[i].wait()
        tiles = []
        for t in range(5):
            at = 640 * i + 128 * t
            tiles.append(a_ref[:, at:at + 128] + b_ref[:, at:at + 128])
            both[0:320, at:at + 128] = tiles[-1]
        middle = tiles[2]
        rolled = pltpu.roll(middle, 64, 1)
        stage[2 * i, 0:320] = tiles[0]
        stage[2 * i, 320:640] = tiles[1]
        stage[2 * i, 640:800] = jnp.where(left, middle[:160], rolled[160:])
        stage[2 * i + 1, 0:320] = tiles[3]
        stage[2 * i + 1, 320:640] = tiles[4]
        stage[2 * i + 1, 640:800] = jnp.where(left, rolled[:160], middle[160:])
    both[320:384] = jnp.zeros((64, both.shape[1]), F32)
    for k, (out, rest) in enumerate(((o0, r0), (o1, r1), (o2, r2), (o3, r3))):
        out[...] = stage[y ^ k, 0:AHEAD]
        rest[0:REST] = stage[y ^ k, AHEAD:800]
    fetch.wait()
    high, low = split(both[...])
    total = dot3(q_buf[...], high, low, NT)
    for rest in (r0, r1, r2, r3):
        rest[REST:REST + 32] = total[:, 0:128]
        rest[REST + 32:REST + 64] = total[:, 128:256]
        rest[REST + 64:REST + 96] = total[:, 256:384] + v_ref[...]


def eliminate(tile):
    lane = lanes((32, 128))
    row = lax.broadcasted_iota(jnp.int32, (32, 128), 0)
    gram = jnp.where((lane >= 64) & (lane < 96), tile, 0.0)
    diagonal = jnp.where(lane == row + 64, gram, 0.0)
    down = lax.rsqrt(jnp.sum(diagonal, axis=1, keepdims=True))
    across = jnp.sum(diagonal, axis=0, keepdims=True)
    across = lax.rsqrt(jnp.where((lane[0:1] >= 64) & (lane[0:1] < 96), across, 1.0))
    work = gram * down * across + jnp.where(lane == row + 96, down, 0.0)
    for k in range(0, 32, 2):
        col0 = jnp.broadcast_to(work[:, 64 + k:65 + k], (32, 128))
        col1 = jnp.broadcast_to(work[:, 65 + k:66 + k], (32, 128))
        a, b, c = col0[k:k + 1], col0[k + 1:k + 2], col1[k + 1:k + 2]
        row0, row1 = work[k:k + 1], work[k + 1:k + 2]
        inverse = 1.0 / (a * c - b * b)
        step0 = (c * row0 - b * row1) * inverse
        step1 = (a * row1 - b * row0) * inverse
        second = jnp.where(row == k + 1, (b * (1.0 / a)) * row0, 0.0)
        work = work - jnp.where(row > k + 1, col0 * step0 + col1 * step1, second)
    pivots = jnp.sum(jnp.where(lane == row + 64, work, 0.0), axis=1, keepdims=True)
    return jnp.where(lane >= 96, work, 0.0), pivots


def below(value):
    return jnp.concatenate([jnp.zeros((96, value.shape[1]), F32), value], axis=0)


def payload(value):
    return jnp.where(lanes(value.shape) < 320, value, 0.0)


def orth(packed):
    inverse, pivots = eliminate(packed[:, 256:384])
    i_high, i_low = split(inverse * lax.rsqrt(pivots))
    b_high, b_low = split(below(payload(packed)))
    return dot(jnp.concatenate([i_high, i_low, i_high], axis=1), jnp.concatenate([b_high, b_high, b_low], axis=0), NN)


def to_right(left, w_high, w_low):
    out = dot3(left, w_high, w_low, NN)
    zero = jnp.zeros((64, left.shape[1]), BF16)
    high, low = (jnp.concatenate([zero, part, zero[:32]], axis=0) for part in split(left))
    return jnp.concatenate([out[:, :256], out[:, 256:] + dot3(left, high, low, NT)], axis=1)


def wide_kernel(m0, m1, m2, m3, p0, p1, p2, p3, high_ref, low_ref, out_ref, vec_ref):
    tail = (p0[...] + p1[...]) + (p2[...] + p3[...])
    whole = unpack(jnp.concatenate([(m0[...] + m1[...]) + (m2[...] + m3[...]), tail[:REST]], axis=0))
    high, low = split(whole)
    zero = jnp.zeros((64, 384), BF16)
    high_ref[...] = jnp.concatenate([high, zero], axis=0)
    low_ref[...] = jnp.concatenate([low, zero], axis=0)
    vec_ref[...] = tail[REST + 64:REST + 96]
    left = payload(jnp.concatenate([tail[REST:REST + 32], tail[REST + 32:REST + 64], tail[REST + 64:REST + 96]], axis=1))
    out_ref[...] = to_right(left, high_ref[...], low_ref[...])


def left_kernel(a0, a1, a2, a3, high_ref, low_ref, out_ref):
    right = orth((a0[...] + a1[...]) + (a2[...] + a3[...]))
    high, low = split(right)
    zero = jnp.zeros((32, 384), BF16)
    w_high = jnp.concatenate([high_ref[0:320], high, zero], axis=0)
    w_low = jnp.concatenate([low_ref[0:320], low, zero], axis=0)
    out_ref[...] = dot3(right, w_high, w_low, NT)


def right_kernel(a0, a1, a2, a3, high_ref, low_ref, left_ref, out_ref):
    left = orth((a0[...] + a1[...]) + (a2[...] + a3[...]))
    left_ref[...] = left
    out_ref[...] = to_right(left, high_ref[...], low_ref[...])


def solve_kernel(packed_ref, left_ref, w_hbm, m_hbm, out_ref, w_out, m_out, sems, *, scale):
    one = pltpu.make_async_copy(w_hbm, w_out, sems.at[0])
    two = pltpu.make_async_copy(m_hbm, m_out, sems.at[1])
    one.start()
    two.start()
    inverse, pivots = eliminate(packed_ref[:, 256:384])
    once = dot(inverse, below(left_ref[...]), NN, HIGH) * (scale / pivots)
    out_ref[...] = dot(inverse, once, TN, HIGH)[96:128]
    one.wait()
    two.wait()


def final_kernel(where, own, other, g0, g1, g2, g3, h0, h1, h2, h3, l_own, l_other, w_ref, m_ref,
                 e_hbm, w_hbm, m_hbm, stage, e_buf, w_buf, m_buf, sems, *, blocks):
    core, y = where[0], where[1]
    size = own.shape[0] // blocks
    side = lanes((32, 128)) < 64
    copies = []
    for slot, (full, left_ref, quarters) in enumerate(
            ((own, l_own, (g0, g1, g2, g3)), (other, l_other, (h0, h1, h2, h3)))):
        mat = core ^ slot
        for k, quarter in enumerate(quarters):
            stage[y ^ k] = quarter[...]
        tiles = []
        for i in range(2):
            even, odd = stage[2 * i], stage[2 * i + 1]
            middle = jnp.where(side, even[:, 256:], pltpu.roll(odd[:, 256:], 64, 1))
            tiles += [even[:, :256], middle, odd[:, :256]]
        r_high, r_low = split(jnp.concatenate(tiles, axis=1))
        l_high, l_low = split(left_ref[...])
        rights = jnp.concatenate([r_high, r_low, r_high], axis=0)
        lefts = jnp.concatenate([l_high, l_high, l_low], axis=0).T
        for block in range(blocks):
            rows = slice(block * size, block * size + size)
            part = dot(lefts[rows], rights, NN)
            e_buf[slot, rows] = full[rows] - part
            moved = 0.9 * m_ref[mat, rows] + part
            m_buf[slot, rows] = moved
            w_buf[slot, rows] = w_ref[mat, rows] - 0.1 * moved
            for j, (buf, hbm) in enumerate(((e_buf, e_hbm), (m_buf, m_hbm), (w_buf, w_hbm))):
                copies.append(pltpu.make_async_copy(buf.at[slot, rows], hbm.at[mat, rows], sems.at[slot, block, j]))
                copies[-1].start()
    for copy in copies:
        copy.wait()


VM = pl.BlockSpec(memory_space=pltpu.VMEM)
SM = pl.BlockSpec(memory_space=pltpu.SMEM)


def limit(mebi):
    return pltpu.CompilerParams(vmem_limit_bytes=mebi << 20)


def shaped(shape, dtype=F32):
    return jax.ShapeDtypeStruct(shape, dtype)


def call(kernel, args, outs, specs, scratch=(), name=None):
    many = isinstance(outs, (list, tuple))
    return pl.pallas_call(
        kernel,
        out_shape=outs,
        in_specs=specs,
        out_specs=[VM] * len(outs) if many else VM,
        scratch_shapes=list(scratch),
        compiler_params=limit(12),
        name=name,
    )(*args)


def gradients(which, acts, cots, errors, scale, name):
    mats, rows, toks = acts.shape
    cols = cots.shape[2]
    step = 512
    inputs = [pltpu.with_memory_space_constraint(value, pltpu.HBM) for value in (acts, cots, errors)]
    return pl.pallas_call(
        lambda *refs: grad_kernel(*refs, scale=scale, step=step, ahead=3),
        out_shape=shaped((rows, cols)),
        in_specs=[SM] + [pl.BlockSpec(memory_space=pltpu.HBM)] * 3,
        out_specs=VM,
        scratch_shapes=[
            pltpu.VMEM((rows, toks), BF16),
            pltpu.VMEM((toks, cols), BF16),
            pltpu.VMEM((rows, cols), F32),
            pltpu.SemaphoreType.DMA((toks // step,)),
            pltpu.SemaphoreType.DMA((toks // step,)),
            pltpu.SemaphoreType.DMA(()),
        ],
        compiler_params=limit(16),
        name=name,
    )(which, *inputs)


def finish(where, own, other, rights, l_own, l_other, weights, momentum):
    blocks = 4
    hbm = pl.BlockSpec(memory_space=pltpu.HBM)
    return pl.pallas_call(
        lambda *refs: final_kernel(*refs, blocks=blocks),
        out_shape=[shaped(weights.shape)] * 3,
        in_specs=[SM] + [VM] * 14,
        out_specs=[hbm] * 3,
        scratch_shapes=[pltpu.VMEM((4, 32, 384), F32)] + [pltpu.VMEM(weights.shape, F32)] * 3
        + [pltpu.SemaphoreType.DMA((2, blocks, 3))],
        compiler_params=limit(24),
        name="finish",
    )(where, own, other, *rights, l_own, l_other, weights, momentum)


def body(acts, cots, errors, weights, momentum, start_q, vec_grads, vec_weights, vec_momentum):
    scale = 1.0 / math.sqrt(acts.shape[1])
    replicas = float(lax.axis_size("replica"))
    index = lax.axis_index("replica")
    core = index & 1
    y = (index >> 1) & 3
    where = jnp.stack([core, y]).astype(jnp.int32)
    acts = acts.swapaxes(1, 2)

    vec_core = vec_grads[0] + swap_core(vec_grads[0])
    other = gradients(1 - where[:1], acts, cots, errors[0], scale, "grad_other")
    own = gradients(where[:1], acts, cots, errors[0], scale, "grad_own")
    vec_core = jnp.pad(vec_core.reshape(20, 64), ((0, 12), (64, 0)))
    hbm = pl.BlockSpec(memory_space=pltpu.HBM)
    in_hbm = lambda value: pltpu.with_memory_space_constraint(value, pltpu.HBM)
    sends = call(route_kernel, (where, own, swap_core(other), in_hbm(start_q.swapaxes(1, 2)), vec_core),
                 [shaped((AHEAD, 128))] * 4 + [shaped((REST + 96, 128))] * 4, [SM, VM, hbm, hbm, VM],
                 [pltpu.VMEM((4, 800, 128), F32), pltpu.VMEM((384, 1280), F32), pltpu.VMEM((320, 1280), F32),
                  pltpu.VMEM((32, 1280), F32), pltpu.SemaphoreType.DMA((2,)), pltpu.SemaphoreType.DMA(())], name="route")
    ahead = add4([sends[0]] + [swap_y(sends[k], k) for k in (1, 2, 3)])
    behind = add4([sends[4]] + [swap_y(sends[4 + k], k) for k in (1, 2, 3)])
    w_high, w_low, packed, vec_sum = call(
        wide_kernel, (*fan(ahead, swap_z), *fan(behind, swap_z)),
        [shaped((384, 384), BF16), shaped((384, 384), BF16), shaped((32, 384)), shaped((32, 128))],
        [VM] * 8, name="first_right")
    packed = call(left_kernel, (*fan(packed, swap_x), w_high, w_low), shaped((32, 384)), [VM] * 6, name="second_left")
    left, packed = call(right_kernel, (*fan(packed, swap_y), w_high, w_low), [shaped((32, 384))] * 2, [VM] * 6,
                        name="second_right")
    packed = add4(fan(packed, swap_x))
    rights = fan(packed, swap_y)
    rights += [swap_core(right) for right in rights]
    held = pltpu.VMEM(weights.shape, F32)
    l_own, weights, momentum = call(
        lambda *refs: solve_kernel(*refs, scale=1.0 / replicas), (rights[0], left, in_hbm(weights), in_hbm(momentum)),
        [shaped((32, 384)), held, held], [VM, VM, hbm, hbm], [pltpu.SemaphoreType.DMA((2,))], name="solve")
    new_errors, new_weights, new_momentum = finish(where, own, other, rights, l_own, swap_core(l_own), weights, momentum)
    vec_moved = 0.9 * vec_momentum + vec_sum[:20, 64:].reshape(4, 320) / replicas
    return (new_errors[None], new_weights, new_momentum, vec_weights - 0.1 * vec_moved, vec_moved)


def solution(mesh):
    placed = (
        P(None, "replica", "shard"),
        P(None, "replica", None),
        P("replica", None, "shard", None),
        P(None, "shard", None),
        P(None, "shard", None),
        P(),
        P("replica", None, "shard"),
        P(None, "shard"),
        P(None, "shard"),
    )
    return jax.shard_map(
        body,
        mesh=mesh,
        in_specs=placed,
        out_specs=(
            P("replica", None, "shard", None),
            P(None, "shard", None),
            P(None, "shard", None),
            P(None, "shard"),
            P(None, "shard"),
        ),
        check_vma=False,
    )
```

```python
import math

import jax
import jax.numpy as jnp
from jax import lax
from jax.experimental import pallas as pl
from jax.experimental.pallas import tpu as pltpu
from jax.sharding import PartitionSpec as P

F32 = jnp.float32
BF16 = jnp.bfloat16
HIGH = lax.Precision.HIGHEST
NN = (((1,), (0,)), ((), ()))
NT = (((1,), (1,)), ((), ()))
TN = (((0,), (0,)), ((), ()))

CORE = [(r, r ^ 1) for r in range(32)]


def swap_core(value):
    return lax.ppermute(value, "replica", CORE)


def swap_y(value, k):
    return lax.ppermute(value, "replica", [(r, r ^ (k << 1)) for r in range(32)])


def swap_z(value, k):
    return lax.ppermute(value, "replica", [(r, r ^ (k << 3)) for r in range(32)])


def swap_x(value, k):
    return lax.ppermute(value, "shard", [(s, s ^ k) for s in range(4)])


def fan(value, swap):
    return [value] + [swap(value, k) for k in (1, 2, 3)]


def add4(parts):
    return (parts[0] + parts[1]) + (parts[2] + parts[3])


def dot(a, b, dims, precision=None):
    return lax.dot_general(a, b, dims, precision=precision, preferred_element_type=F32)


def split(value):
    high = value.astype(BF16)
    return high, (value - high.astype(F32)).astype(BF16)


def dot3(a, b_high, b_low, dims):
    high, low = split(a)
    rows = a.shape[0]
    top = dot(jnp.concatenate([high, low], axis=0), b_high, dims)
    return top[:rows] + (top[rows:] + dot(high, b_low, dims))


def lanes(shape):
    return lax.broadcasted_iota(jnp.int32, shape, 1)


def unpack(chunk):
    half = chunk[640:800]
    half = jnp.concatenate([half, pltpu.roll(half, 64, 1)], axis=0)
    half = jnp.where(lanes(half.shape) < 64, half, 0.0)
    return jnp.concatenate([chunk[:320], chunk[320:640], half], axis=1)


def grad_kernel(which, a_hbm, c_hbm, e_hbm, out_ref, a_buf, c_buf, e_buf, a_sem, c_sem, e_sem, *, scale, step, ahead):
    mat = which[0]
    blocks = [pl.ds(at, step) for at in range(0, c_buf.shape[0], step)]
    lhs = [pltpu.make_async_copy(a_hbm.at[mat, :, b], a_buf.at[:, b], a_sem.at[j]) for j, b in enumerate(blocks)]
    rhs = [pltpu.make_async_copy(c_hbm.at[mat, b], c_buf.at[b], c_sem.at[j]) for j, b in enumerate(blocks)]
    kept = pltpu.make_async_copy(e_hbm.at[mat], e_buf, e_sem)
    last = len(blocks) - 1

    def start(j):
        if j <= last:
            lhs[j].start()
            rhs[j].start()
        if j == last:
            kept.start()

    for j in range(ahead):
        start(j)
    for j, b in enumerate(blocks):
        lhs[j].wait()
        rhs[j].wait()
        start(j + ahead)
        value = dot(a_buf[:, b], c_buf[b], NN)
        if j == last:
            kept.wait()
            out_ref[...] = (out_ref[...] + value) * scale + e_buf[...]
        elif j > 0:
            out_ref[...] = out_ref[...] + value
        else:
            out_ref[...] = value


AHEAD = 448
REST = 800 - AHEAD


def route_kernel(where, a_ref, b_hbm, q_hbm, v_ref, o0, o1, o2, o3, r0, r1, r2, r3, stage, both, b_ref, q_buf, b_sem, q_sem):
    core, y = where[0], where[1]
    fetch = pltpu.make_async_copy(q_hbm.at[core], q_buf, q_sem)
    halves = [pltpu.make_async_copy(b_hbm.at[:, at:at + 640], b_ref.at[:, at:at + 640], b_sem.at[i])
              for i, at in enumerate((0, 640))]
    halves[0].start()
    halves[1].start()
    fetch.start()
    left = lanes((160, 128)) < 64
    for i in range(2):
        halves[i].wait()
        tiles = []
        for t in range(5):
            at = 640 * i + 128 * t
            tiles.append(a_ref[:, at:at + 128] + b_ref[:, at:at + 128])
            both[0:320, at:at + 128] = tiles[-1]
        middle = tiles[2]
        rolled = pltpu.roll(middle, 64, 1)
        stage[2 * i, 0:320] = tiles[0]
        stage[2 * i, 320:640] = tiles[1]
        stage[2 * i, 640:800] = jnp.where(left, middle[:160], rolled[160:])
        stage[2 * i + 1, 0:320] = tiles[3]
        stage[2 * i + 1, 320:640] = tiles[4]
        stage[2 * i + 1, 640:800] = jnp.where(left, rolled[:160], middle[160:])
    both[320:384] = jnp.zeros((64, both.shape[1]), F32)
    for k, (out, rest) in enumerate(((o0, r0), (o1, r1), (o2, r2), (o3, r3))):
        out[...] = stage[y ^ k, 0:AHEAD]
        rest[0:REST] = stage[y ^ k, AHEAD:800]
    fetch.wait()
    high, low = split(both[...])
    total = dot3(q_buf[...], high, low, NT)
    for rest in (r0, r1, r2, r3):
        rest[REST:REST + 32] = total[:, 0:128]
        rest[REST + 32:REST + 64] = total[:, 128:256]
        rest[REST + 64:REST + 96] = total[:, 256:384] + v_ref[...]


def eliminate(tile):
    lane = lanes((32, 128))
    row = lax.broadcasted_iota(jnp.int32, (32, 128), 0)
    gram = jnp.where((lane >= 64) & (lane < 96), tile, 0.0)
    diagonal = jnp.where(lane == row + 64, gram, 0.0)
    down = lax.rsqrt(jnp.sum(diagonal, axis=1, keepdims=True))
    across = jnp.sum(diagonal, axis=0, keepdims=True)
    across = lax.rsqrt(jnp.where((lane[0:1] >= 64) & (lane[0:1] < 96), across, 1.0))
    work = gram * down * across + jnp.where(lane == row + 96, down, 0.0)
    for k in range(0, 32, 2):
        col0 = jnp.broadcast_to(work[:, 64 + k:65 + k], (32, 128))
        col1 = jnp.broadcast_to(work[:, 65 + k:66 + k], (32, 128))
        a, b, c = col0[k:k + 1], col0[k + 1:k + 2], col1[k + 1:k + 2]
        row0, row1 = work[k:k + 1], work[k + 1:k + 2]
        inverse = 1.0 / (a * c - b * b)
        step0 = (c * row0 - b * row1) * inverse
        step1 = (a * row1 - b * row0) * inverse
        second = jnp.where(row == k + 1, (b * (1.0 / a)) * row0, 0.0)
        work = work - jnp.where(row > k + 1, col0 * step0 + col1 * step1, second)
    pivots = jnp.sum(jnp.where(lane == row + 64, work, 0.0), axis=1, keepdims=True)
    return jnp.where(lane >= 96, work, 0.0), pivots


def below(value):
    return jnp.concatenate([jnp.zeros((96, value.shape[1]), F32), value], axis=0)


def payload(value):
    return jnp.where(lanes(value.shape) < 320, value, 0.0)


def orth(packed):
    inverse, pivots = eliminate(packed[:, 256:384])
    i_high, i_low = split(inverse * lax.rsqrt(pivots))
    b_high, b_low = split(below(payload(packed)))
    return dot(jnp.concatenate([i_high, i_low, i_high], axis=1), jnp.concatenate([b_high, b_high, b_low], axis=0), NN)


def to_right(left, w_high, w_low):
    out = dot3(left, w_high, w_low, NN)
    zero = jnp.zeros((64, left.shape[1]), BF16)
    high, low = (jnp.concatenate([zero, part, zero[:32]], axis=0) for part in split(left))
    return jnp.concatenate([out[:, :256], out[:, 256:] + dot3(left, high, low, NT)], axis=1)


def wide_kernel(m0, m1, m2, m3, p0, p1, p2, p3, high_ref, low_ref, out_ref, vec_ref):
    tail = (p0[...] + p1[...]) + (p2[...] + p3[...])
    whole = unpack(jnp.concatenate([(m0[...] + m1[...]) + (m2[...] + m3[...]), tail[:REST]], axis=0))
    high, low = split(whole)
    zero = jnp.zeros((64, 384), BF16)
    high_ref[...] = jnp.concatenate([high, zero], axis=0)
    low_ref[...] = jnp.concatenate([low, zero], axis=0)
    vec_ref[...] = tail[REST + 64:REST + 96]
    left = payload(jnp.concatenate([tail[REST:REST + 32], tail[REST + 32:REST + 64], tail[REST + 64:REST + 96]], axis=1))
    out_ref[...] = to_right(left, high_ref[...], low_ref[...])


def left_kernel(a0, a1, a2, a3, high_ref, low_ref, out_ref):
    right = orth((a0[...] + a1[...]) + (a2[...] + a3[...]))
    high, low = split(right)
    zero = jnp.zeros((32, 384), BF16)
    w_high = jnp.concatenate([high_ref[0:320], high, zero], axis=0)
    w_low = jnp.concatenate([low_ref[0:320], low, zero], axis=0)
    out_ref[...] = dot3(right, w_high, w_low, NT)


def right_kernel(a0, a1, a2, a3, high_ref, low_ref, left_ref, out_ref):
    left = orth((a0[...] + a1[...]) + (a2[...] + a3[...]))
    left_ref[...] = left
    out_ref[...] = to_right(left, high_ref[...], low_ref[...])


def solve_kernel(where, packed_ref, left_ref, w_hbm, m_hbm, out_ref, w_out, m_out, sems, *, scale):
    one = pltpu.make_async_copy(w_hbm.at[where[0]], w_out, sems.at[0])
    two = pltpu.make_async_copy(m_hbm, m_out, sems.at[1])
    one.start()
    two.start()
    inverse, pivots = eliminate(packed_ref[:, 256:384])
    once = dot(inverse, below(left_ref[...]), NN, HIGH) * (scale / pivots)
    out_ref[...] = dot(inverse, once, TN, HIGH)[96:128]
    one.wait()
    two.wait()


def final_kernel(where, own, other, g0, g1, g2, g3, h0, h1, h2, h3, l_own, l_other, w_ref, m_ref, w_in,
                 e_hbm, w_hbm, m_hbm, stage, e_buf, w_buf, m_buf, w_rest, sems, w_sem, *, blocks):
    core, y = where[0], where[1]
    size = own.shape[0] // blocks
    side = lanes((32, 128)) < 64
    fetch = pltpu.make_async_copy(w_in.at[1 - core], w_rest, w_sem)
    fetch.start()
    copies = []
    for slot, (full, left_ref, quarters) in enumerate(
            ((own, l_own, (g0, g1, g2, g3)), (other, l_other, (h0, h1, h2, h3)))):
        mat = core ^ slot
        held = (w_ref, w_rest)[slot]
        if slot == 1:
            fetch.wait()
        for k, quarter in enumerate(quarters):
            stage[y ^ k] = quarter[...]
        tiles = []
        for i in range(2):
            even, odd = stage[2 * i], stage[2 * i + 1]
            middle = jnp.where(side, even[:, 256:], pltpu.roll(odd[:, 256:], 64, 1))
            tiles += [even[:, :256], middle, odd[:, :256]]
        r_high, r_low = split(jnp.concatenate(tiles, axis=1))
        l_high, l_low = split(left_ref[...])
        rights = jnp.concatenate([r_high, r_low, r_high], axis=0)
        lefts = jnp.concatenate([l_high, l_high, l_low], axis=0).T
        for block in range(blocks):
            rows = slice(block * size, block * size + size)
            part = dot(lefts[rows], rights, NN)
            e_buf[slot, rows] = full[rows] - part
            moved = 0.9 * m_ref[mat, rows] + part
            m_buf[slot, rows] = moved
            w_buf[slot, rows] = held[rows] - 0.1 * moved
            for j, (buf, hbm) in enumerate(((e_buf, e_hbm), (m_buf, m_hbm), (w_buf, w_hbm))):
                copies.append(pltpu.make_async_copy(buf.at[slot, rows], hbm.at[mat, rows], sems.at[slot, block, j]))
                copies[-1].start()
    for copy in copies:
        copy.wait()


VM = pl.BlockSpec(memory_space=pltpu.VMEM)
SM = pl.BlockSpec(memory_space=pltpu.SMEM)


def limit(mebi):
    return pltpu.CompilerParams(vmem_limit_bytes=mebi << 20)


def shaped(shape, dtype=F32):
    return jax.ShapeDtypeStruct(shape, dtype)


def call(kernel, args, outs, specs, scratch=(), name=None):
    many = isinstance(outs, (list, tuple))
    return pl.pallas_call(
        kernel,
        out_shape=outs,
        in_specs=specs,
        out_specs=[VM] * len(outs) if many else VM,
        scratch_shapes=list(scratch),
        compiler_params=limit(12),
        name=name,
    )(*args)


def gradients(which, acts, cots, errors, scale, name):
    mats, rows, toks = acts.shape
    cols = cots.shape[2]
    step = 512
    inputs = [pltpu.with_memory_space_constraint(value, pltpu.HBM) for value in (acts, cots, errors)]
    return pl.pallas_call(
        lambda *refs: grad_kernel(*refs, scale=scale, step=step, ahead=3),
        out_shape=shaped((rows, cols)),
        in_specs=[SM] + [pl.BlockSpec(memory_space=pltpu.HBM)] * 3,
        out_specs=VM,
        scratch_shapes=[
            pltpu.VMEM((rows, toks), BF16),
            pltpu.VMEM((toks, cols), BF16),
            pltpu.VMEM((rows, cols), F32),
            pltpu.SemaphoreType.DMA((toks // step,)),
            pltpu.SemaphoreType.DMA((toks // step,)),
            pltpu.SemaphoreType.DMA(()),
        ],
        compiler_params=limit(16),
        name=name,
    )(which, *inputs)


def finish(where, own, other, rights, l_own, l_other, own_weights, momentum, weights):
    blocks = 4
    hbm = pl.BlockSpec(memory_space=pltpu.HBM)
    return pl.pallas_call(
        lambda *refs: final_kernel(*refs, blocks=blocks),
        out_shape=[shaped(weights.shape)] * 3,
        in_specs=[SM] + [VM] * 14 + [hbm],
        out_specs=[hbm] * 3,
        scratch_shapes=[pltpu.VMEM((4, 32, 384), F32)] + [pltpu.VMEM(weights.shape, F32)] * 3
        + [pltpu.VMEM(weights.shape[1:], F32), pltpu.SemaphoreType.DMA((2, blocks, 3)), pltpu.SemaphoreType.DMA(())],
        compiler_params=limit(24),
        name="finish",
    )(where, own, other, *rights, l_own, l_other, own_weights, momentum, weights)


def body(acts, cots, errors, weights, momentum, start_q, vec_grads, vec_weights, vec_momentum):
    scale = 1.0 / math.sqrt(acts.shape[1])
    replicas = float(lax.axis_size("replica"))
    index = lax.axis_index("replica")
    core = index & 1
    y = (index >> 1) & 3
    where = jnp.stack([core, y]).astype(jnp.int32)
    acts = acts.swapaxes(1, 2)

    vec_core = vec_grads[0] + swap_core(vec_grads[0])
    other = gradients(1 - where[:1], acts, cots, errors[0], scale, "grad_other")
    own = gradients(where[:1], acts, cots, errors[0], scale, "grad_own")
    vec_core = jnp.pad(vec_core.reshape(20, 64), ((0, 12), (64, 0)))
    hbm = pl.BlockSpec(memory_space=pltpu.HBM)
    in_hbm = lambda value: pltpu.with_memory_space_constraint(value, pltpu.HBM)
    sends = call(route_kernel, (where, own, swap_core(other), in_hbm(start_q.swapaxes(1, 2)), vec_core),
                 [shaped((AHEAD, 128))] * 4 + [shaped((REST + 96, 128))] * 4, [SM, VM, hbm, hbm, VM],
                 [pltpu.VMEM((4, 800, 128), F32), pltpu.VMEM((384, 1280), F32), pltpu.VMEM((320, 1280), F32),
                  pltpu.VMEM((32, 1280), F32), pltpu.SemaphoreType.DMA((2,)), pltpu.SemaphoreType.DMA(())], name="route")
    ahead = add4([sends[0]] + [swap_y(sends[k], k) for k in (1, 2, 3)])
    behind = add4([sends[4]] + [swap_y(sends[4 + k], k) for k in (1, 2, 3)])
    w_high, w_low, packed, vec_sum = call(
        wide_kernel, (*fan(ahead, swap_z), *fan(behind, swap_z)),
        [shaped((384, 384), BF16), shaped((384, 384), BF16), shaped((32, 384)), shaped((32, 128))],
        [VM] * 8, name="first_right")
    packed = call(left_kernel, (*fan(packed, swap_x), w_high, w_low), shaped((32, 384)), [VM] * 6, name="second_left")
    left, packed = call(right_kernel, (*fan(packed, swap_y), w_high, w_low), [shaped((32, 384))] * 2, [VM] * 6,
                        name="second_right")
    packed = add4(fan(packed, swap_x))
    rights = fan(packed, swap_y)
    rights += [swap_core(right) for right in rights]
    weights = in_hbm(weights)
    l_own, own_weights, momentum = call(
        lambda *refs: solve_kernel(*refs, scale=1.0 / replicas), (where, rights[0], left, weights, in_hbm(momentum)),
        [shaped((32, 384)), pltpu.VMEM(weights.shape[1:], F32), pltpu.VMEM(weights.shape, F32)], [SM, VM, VM, hbm, hbm],
        [pltpu.SemaphoreType.DMA((2,))], name="solve")
    new_errors, new_weights, new_momentum = finish(where, own, other, rights, l_own, swap_core(l_own), own_weights, momentum,
                                                   weights)
    vec_moved = 0.9 * vec_momentum + vec_sum[:20, 64:].reshape(4, 320) / replicas
    return (new_errors[None], new_weights, new_momentum, vec_weights - 0.1 * vec_moved, vec_moved)


def solution(mesh):
    placed = (
        P(None, "replica", "shard"),
        P(None, "replica", None),
        P("replica", None, "shard", None),
        P(None, "shard", None),
        P(None, "shard", None),
        P(),
        P("replica", None, "shard"),
        P(None, "shard"),
        P(None, "shard"),
    )
    return jax.shard_map(
        body,
        mesh=mesh,
        in_specs=placed,
        out_specs=(
            P("replica", None, "shard", None),
            P(None, "shard", None),
            P(None, "shard", None),
            P(None, "shard"),
            P(None, "shard"),
        ),
        check_vma=False,
    )
```
